768 devices in a mesh: pos: 96 (over y, z), col: 8 (over x, core).
Axes of the slice: x: 4, y: 8, z: 12, core: 2. Of those that a mesh axis runs over, the one named last changes fastest.
Arguments:
- object_layers: float32 [2, 2, 768, 768], P(None, None, 'pos', 'col'), may hold values from -6 to 6
- probe_field: float32 [2, 256, 256], P(None, 'col'), may hold values from -6 to 6
- prop_phase: float32 [256, 256], P(None, 'col'), may hold values from -3.140625 to 3.140625
- amplitude: float32 [96, 256, 256], P('pos', None, 'col'), may hold values from 0 to 2
- offsets: int32 [96, 2], P('pos'), may hold values from 0 to 512
- counts: int32 [96], P('pos'), may hold values from 1 to 1, as said below
Outputs:
- object_grad: float32 [2, 2, 768, 768], P(None, None, 'pos', 'col')
The draws below stay inside these ranges and needn't reach their ends.
Inputs may be any that keep to these rules, and one draw needn't show every extreme that they name: `counts`: slots of a pos index at or above its count are padding; some index of pos is full in every draw.
All inputs are finite; a program needn't handle non-finite values.
Results may differ from the reference program's by a relative error of at most 0.0003.
Values sent between devices are 32-bit elements; how exact they have to be, the bound alone decides.
No kernel may reach another device: no remote copies, remote signals or barrier semaphores. Data moves between devices by JAX's collectives and lax.ppermute only.
A program may use at most 32 MiB of HBM per device.

```python
import jax
import jax.numpy as jnp
from jax import lax

P_SIZE = 256
NOBJ = 768
LAYERS = 2
POS_DEV = 1
POSITIONS = 96
N_POS = 96


def draw_counts(key, part):
    first_key = jax.random.fold_in(key, 11)
    second_key = jax.random.fold_in(key, 23)
    values = jax.random.randint(first_key, (N_POS,), 1, POS_DEV + 1, dtype=jnp.int32)
    chosen = jax.random.randint(second_key, (), 0, N_POS, dtype=jnp.int32)
    return values.at[chosen].set(POS_DEV)


def place_ends(values, rng, low, top_value):
    spot = [jax.random.randint(jax.random.fold_in(rng, axis), (), 0, length) for axis, length in enumerate(values.shape)]
    widest = values.shape.index(max(values.shape))
    neighbour = spot[:widest] + [(spot[widest] + 1) % values.shape[widest]] + spot[widest + 1:]
    return values.at[tuple(spot)].set(low).at[tuple(neighbour)].set(top_value)


def level_of(key, extent, cuts, smallest, top_value):
    def one(axis_at, shards_of):
        heights = jax.random.uniform(jax.random.fold_in(jax.random.fold_in(key, 6), axis_at), (shards_of,), jnp.float32, smallest / len(cuts), top_value / len(cuts))
        return jnp.repeat(jnp.exp(heights), extent[axis_at] // shards_of).reshape((-1,) + (1,) * (len(extent) - axis_at - 1))

    gain = one(*cuts[0])
    for cut in cuts[1:]:
        gain = gain * one(*cut)
    return gain


def normal_values(key, extent, width, bound, shards=(), held_as=jnp.bfloat16):
    drawn = jax.random.normal(key, extent, jnp.float32) * width
    if len(shards) > 0:
        drawn = level_of(key, extent, shards, -0.22, 0.18) * drawn
    return jnp.clip(drawn, min=-bound, max=bound).astype(held_as)


def setup_inputs(seed: int = 0) -> dict:
    seeds = jax.random.split(jax.random.key(seed), 7)
    return {
        "object_layers": normal_values(seeds[0], (LAYERS, 2, NOBJ, NOBJ), 1.0, 6.0, ((2, 96), (3, 8)), jnp.float32),
        "probe_field": normal_values(seeds[1], (2, P_SIZE, P_SIZE), 1.0, 6.0, ((1, 8),), jnp.float32),
        "prop_phase": jnp.clip(jax.random.uniform(seeds[2], (P_SIZE, P_SIZE), jnp.float32, -3.140625, 3.140625), -3.140625, 3.140625),
        "amplitude": jnp.clip(2.0 * jax.random.uniform(seeds[3], (POSITIONS, P_SIZE, P_SIZE), jnp.float32) ** level_of(seeds[3], (POSITIONS, P_SIZE, P_SIZE), ((0, 96), (2, 8)), -0.2, 0.2), 0.0, 2.0),
        "offsets": place_ends(jax.random.randint(seeds[4], (POSITIONS, 2), 0, NOBJ - P_SIZE + 1), jax.random.fold_in(seeds[4], 1), 0, NOBJ - P_SIZE).astype(jnp.int32),
        "counts": draw_counts(jax.random.fold_in(seeds[6], 71), 0),
    }


MOD_FLOOR = 0.1


def transform(field_data):
    return jnp.fft.fft2(field_data, norm="ortho")


def untransform(field_data):
    return jnp.fft.ifft2(field_data, norm="ortho")


def reference(object_layers, probe_field, prop_phase, amplitude, offsets, counts):
    probe_complex = probe_field[0] + 1j * probe_field[1]
    kernel = jnp.cos(prop_phase) + 1j * jnp.sin(prop_phase)
    slot_ids = jnp.arange(POSITIONS, dtype=jnp.int32)
    alive_mask = (slot_ids % POS_DEV < counts[slot_ids // POS_DEV]).astype(jnp.float32)
    zero_index = jnp.zeros((), jnp.int32)

    def one_position(grad_total, position):
        row_at = offsets[position, 0].astype(jnp.int32)
        col_at = offsets[position, 1].astype(jnp.int32)
        corner = (zero_index, zero_index, row_at, col_at)
        patch_set = lax.dynamic_slice(object_layers, corner, (LAYERS, 2, P_SIZE, P_SIZE))
        layer_complex = patch_set[:, 0] + 1j * patch_set[:, 1]
        wave_now = probe_complex * layer_complex[0]
        wave_list = []
        for layer_idx in range(1, LAYERS):
            propagated = untransform(kernel * transform(wave_now))
            wave_list.append(propagated)
            wave_now = propagated * layer_complex[layer_idx]
        far_field = transform(wave_now)
        modulus = jnp.maximum(jnp.abs(far_field), MOD_FLOOR)
        residual = far_field - amplitude[position] * far_field / modulus
        backward = untransform(residual)
        gradients = [None] * LAYERS
        for layer_idx in range(LAYERS - 1, 0, -1):
            gradients[layer_idx] = jnp.conj(wave_list[layer_idx - 1]) * backward
            toward = jnp.conj(layer_complex[layer_idx]) * backward
            backward = untransform(jnp.conj(kernel) * transform(toward))
        gradients[0] = jnp.conj(probe_complex) * backward
        stacked = jnp.stack([jnp.stack([grad_item.real, grad_item.imag]) for grad_item in gradients])
        stacked = stacked.astype(grad_total.dtype) * alive_mask[position].astype(grad_total.dtype)
        current = lax.dynamic_slice(grad_total, corner, (LAYERS, 2, P_SIZE, P_SIZE))
        grad_total = lax.dynamic_update_slice(grad_total, current + stacked, corner)
        return grad_total, None

    start_total = jnp.zeros(object_layers.shape, object_layers.dtype)
    grad_total, unused = lax.scan(one_position, start_total, jnp.arange(POSITIONS, dtype=jnp.int32))
    return grad_total
```

```python
import functools

import jax
import jax.numpy as jnp
import numpy as np
from jax import lax
from jax.experimental import pallas as pl
from jax.experimental.pallas import tpu as pltpu
from jax.sharding import Mesh
from jax.sharding import PartitionSpec as P

POS = ("pos_0", "pos_1")
MOD_FLOOR = 0.1

Y, Z, C = 8, 12, 8
N = 256
PLANES = 4
TILE = 8
CLASS_IN_STRIP = 12
CLASS_IN_PATCH = 32
TILES_PER_Z = 3
LANES = 128
VMEM_LIMIT = 60 * 1024 * 1024
F32 = jnp.float32
BF16 = jnp.bfloat16


def exchange(x, axes):
    return lax.all_to_all(x, axes, 0, 0, tiled=True)


def class_order():
    table = np.zeros((C * CLASS_IN_STRIP, LANES), np.float32)
    for j in range(C):
        for u in range(CLASS_IN_STRIP):
            table[C * u + j, 16 * j + u] = 1.0
    return table


def dft_tables():
    counter = np.arange(N)
    angle = (counter[:, None] * counter[None, :] % N) * (2.0 * np.pi / N)
    cosine, sine = np.cos(angle) / 16.0, np.sin(angle) / 16.0
    parts = []
    for table in (cosine, cosine + sine, cosine - sine):
        table = table.astype(np.float32)
        high = table.astype(jnp.bfloat16)
        low = (table - high.astype(np.float32)).astype(jnp.bfloat16)
        parts += [high, low]
    return np.stack(parts)


def lanes():
    return lax.broadcasted_iota(jnp.int32, (TILE, LANES), 1)


def between(lane, low, width):
    return (lane >= low) & (lane < low + width)


def rolled(x, shift):
    if isinstance(shift, int):
        shift = shift % LANES
        return pltpu.roll(x, shift, 1) if shift else x
    return pltpu.roll(x, lax.rem(shift + LANES, LANES), 1)


def split_kernel(x_ref, order_ref, o_ref):
    tile = x_ref[...].reshape(PLANES * TILE, C * CLASS_IN_STRIP)
    ordered = jnp.dot(
        tile, order_ref[...], precision=lax.Precision.HIGHEST, preferred_element_type=F32
    )
    lane = lanes()
    for j in range(C):
        piece = jnp.zeros((TILE, LANES), F32)
        for p in range(PLANES):
            moved = rolled(ordered[p * TILE : (p + 1) * TILE], 32 * p - 16 * j)
            piece = jnp.where(between(lane, 32 * p, CLASS_IN_STRIP), moved, piece)
        for y in range(Y):
            o_ref[y * C + j] = piece


def window(off_ref, me_ref, z):
    row, col = off_ref[z, 0], off_ref[z, 1]
    z_me, c_me = me_ref[0], me_ref[1]
    first = lax.shift_right_logical(row, 3)
    ahead = lax.rem(z_me - first + 6 * Z, Z)
    y_first = lax.div(first + ahead - z_me, Z)
    u_first = lax.shift_right_logical(col - c_me + 7, 3)
    return y_first, u_first


def select_kernel(off_ref, me_ref, x_ref, o_ref, strip_ref):
    lane = lanes()
    for y in range(Y):
        for p in range(PLANES):
            line = jnp.zeros((TILE, LANES), F32)
            for j in range(C):
                moved = rolled(x_ref[y * C + j], CLASS_IN_STRIP * j - 32 * p)
                line = jnp.where(between(lane, CLASS_IN_STRIP * j, CLASS_IN_STRIP), moved, line)
            strip_ref[p, y] = line
    for p in range(PLANES):
        strip_ref[p, Y] = jnp.zeros((TILE, LANES), F32)
    for z in range(Z):
        y_first, u_first = window(off_ref, me_ref, z)
        for k in range(TILES_PER_Z):
            piece = jnp.zeros((TILE, LANES), F32)
            for p in range(PLANES):
                moved = rolled(strip_ref[p, y_first + k], 32 * p - u_first)
                piece = jnp.where(between(lane, 32 * p, CLASS_IN_PATCH), moved, piece)
            o_ref[z, k * TILE : (k + 1) * TILE] = piece


def pack_kernel(own_ref, x_ref, phase_ref, amp_ref, probe_ref, o_ref, rows_ref):
    row = own_ref[0]
    first = lax.shift_right_logical(row, 3)
    for m in range(Z * TILES_PER_Z):
        k = m // Z
        rows_ref[m * TILE : (m + 1) * TILE] = x_ref[
            lax.rem(first + m, Z), k * TILE : (k + 1) * TILE
        ]
    patch = rows_ref[pl.ds(row & 7, N), :].T
    for copy in range(C):
        o_ref[copy, 0:128] = patch
        o_ref[copy, 128:160] = phase_ref[...]
        o_ref[copy, 160:192] = amp_ref[...]
        o_ref[copy, 192:224] = probe_ref[0]
        o_ref[copy, 224:256] = probe_ref[1]


def two_terms(x):
    high = x.astype(BF16)
    return high, (x - high.astype(F32)).astype(BF16)


def product(first, second):
    def dot(a, b):
        return jnp.dot(a, b, preferred_element_type=F32)

    return dot(first[0], second[0]) + (dot(first[0], second[1]) + dot(first[1], second[0]))


def store(ref, at, value):
    ref[at, 0] = value[:, :LANES]
    ref[at, 1] = value[:, LANES:]


def load(ref, at, rows=slice(None)):
    return jnp.concatenate([ref[at, 0, rows, :], ref[at, 1, rows, :]], axis=1)


def main_kernel(
    own_ref, me_ref, g_ref, tab_ref, o_ref, patch_ref, h_ref, amp_ref, probe_ref, wave_ref, x_ref, rows_ref
):
    row, col, count = own_ref[0], own_ref[1], own_ref[2]
    for s in range(C):
        source = lax.rem(col + s, C)
        for p in range(PLANES):
            for half in range(2):
                patch_ref[p, half, pl.ds(s, CLASS_IN_PATCH, stride=C), :] = g_ref[
                    source, p * 32 : (p + 1) * 32, half * LANES : (half + 1) * LANES
                ]
    phase = g_ref[:, 128:160, :].reshape(N, N)
    store(h_ref, 0, jnp.cos(phase))
    store(h_ref, 1, jnp.sin(phase))
    amp_ref[...] = g_ref[:, 160:192, :].reshape(N, N)
    store(probe_ref, 0, g_ref[:, 192:224, :].reshape(N, N).T)
    store(probe_ref, 1, g_ref[:, 224:256, :].reshape(N, N).T)

    def table(k):
        return tab_ref[2 * k], tab_ref[2 * k + 1]

    def held(ref, at=0, rows=slice(None)):
        return load(ref, at, rows), load(ref, at + 1, rows)

    def keep(ref, pair):
        store(ref, 0, pair[0])
        store(ref, 1, pair[1])

    def transform(pair, inverse):
        real_table, imag_table = (1, 2) if inverse else (2, 1)
        for left in (False, True):
            real, imag = pair
            both = two_terms(real + imag)
            real, imag = two_terms(real), two_terms(imag)

            def times(data, k):
                return product(table(k), data) if left else product(data, table(k))

            common = times(both, 0)
            keep(x_ref, (common - times(imag, real_table), common - times(real, imag_table)))
            pair = held(x_ref)
        return pair

    def times(a, b):
        return a[0] * b[0] - a[1] * b[1], a[0] * b[1] + a[1] * b[0]

    def conj_times(a, b):
        return a[0] * b[0] + a[1] * b[1], a[0] * b[1] - a[1] * b[0]

    spectrum = transform(times(held(probe_ref), held(patch_ref)), False)
    wave = transform(times(held(h_ref), spectrum), True)
    keep(wave_ref, wave)
    far = transform(times(held(wave_ref), held(patch_ref, 2)), False)
    modulus = jnp.maximum(jnp.sqrt(far[0] * far[0] + far[1] * far[1]), MOD_FLOOR)
    ratio = amp_ref[...] / modulus
    back = transform((far[0] - ratio * far[0], far[1] - ratio * far[1]), True)
    keep(wave_ref, conj_times(held(wave_ref), back))
    toward = transform(conj_times(held(patch_ref, 2), back), False)
    transform(conj_times(held(h_ref), toward), True)

    mine = pl.ds(lax.rem(me_ref[1] - col + 1024, C), CLASS_IN_PATCH, stride=C)
    first_grad = conj_times(held(probe_ref, 0, mine), held(x_ref, 0, mine))
    second_grad = held(wave_ref, 0, mine)
    alive = (count > 0).astype(F32)
    grads = jnp.concatenate([*first_grad, *second_grad], axis=0) * alive
    rows_ref[...] = jnp.zeros_like(rows_ref)
    rows_ref[pl.ds(row & 7, N), :] = grads.T
    first = lax.shift_right_logical(row, 3)
    for m in range(Z * TILES_PER_Z):
        k = m // Z
        o_ref[lax.rem(first + m, Z), k * TILE : (k + 1) * TILE] = rows_ref[
            m * TILE : (m + 1) * TILE
        ]


def gather_kernel(off_ref, me_ref, x_ref, o_ref, sum_ref):
    lane = lanes()
    sum_ref[...] = jnp.zeros_like(sum_ref)
    for z in range(Z):
        y_first, u_first = window(off_ref, me_ref, z)
        inside = between(lane, u_first, CLASS_IN_PATCH)
        for k in range(TILES_PER_Z):
            piece = x_ref[z, k * TILE : (k + 1) * TILE]
            for p in range(PLANES):
                moved = jnp.where(inside, rolled(piece, u_first - 32 * p), 0.0)
                sum_ref[p, y_first + k] += moved
    for y in range(Y):
        for j in range(C):
            piece = jnp.zeros((TILE, LANES), F32)
            for p in range(PLANES):
                moved = rolled(sum_ref[p, y], 32 * p - CLASS_IN_STRIP * j)
                piece = jnp.where(between(lane, 32 * p, CLASS_IN_STRIP), moved, piece)
            o_ref[y * C + j] = piece


def merge_kernel(x_ref, order_ref, o_ref):
    lane = lanes()
    sums = []
    for j in range(C):
        total = x_ref[j]
        for y in range(1, Y):
            total = total + x_ref[y * C + j]
        sums.append(total)
    planes = []
    for p in range(PLANES):
        line = jnp.zeros((TILE, LANES), F32)
        for j in range(C):
            line = jnp.where(
                between(lane, 16 * j, CLASS_IN_STRIP), rolled(sums[j], 16 * j - 32 * p), line
            )
        planes.append(line)
    ordered = jnp.concatenate(planes, axis=0)
    tile = jnp.dot(
        ordered, order_ref[...], precision=lax.Precision.HIGHEST, preferred_element_type=F32
    )
    o_ref[...] = tile.reshape(2, 2, TILE, C * CLASS_IN_STRIP)


IN_VMEM = pl.BlockSpec(memory_space=pltpu.VMEM)
IN_SMEM = pl.BlockSpec(memory_space=pltpu.SMEM)


def call(kernel, out_shape, scalars, arrays, scratch=()):
    return pl.pallas_call(
        kernel,
        out_shape=jax.ShapeDtypeStruct(out_shape, F32),
        in_specs=[IN_SMEM] * len(scalars) + [IN_VMEM] * len(arrays),
        out_specs=IN_VMEM,
        scratch_shapes=[pltpu.VMEM(shape, F32) for shape in scratch],
        compiler_params=pltpu.CompilerParams(vmem_limit_bytes=VMEM_LIMIT),
    )(*scalars, *arrays)


def per_device(object_layers, probe_field, prop_phase, amplitude, offsets, counts):
    order = class_order()
    me = jnp.stack([lax.axis_index("pos_1"), lax.axis_index("col")]).astype(jnp.int32)
    own = jnp.concatenate([offsets[0], counts])
    line_offsets = exchange(jnp.broadcast_to(offsets[None], (Z, 1, 2)), "pos_1").reshape(Z, 2)
    split = call(split_kernel, (Y * C, TILE, LANES), (), (object_layers, jnp.asarray(order)))
    columns = exchange(split, ("pos_0", "col"))
    strip_shape = (PLANES, Y + 1, TILE, LANES)
    piece_shape = (Z, TILES_PER_Z * TILE, LANES)
    halves = (2, N, LANES)
    rows_shape = (Z * TILES_PER_Z * TILE + TILE, LANES)
    chosen = call(select_kernel, piece_shape, (line_offsets, me), (columns,), (strip_shape,))
    rows = exchange(chosen, "pos_1")
    packed = call(
        pack_kernel,
        (C, N, N),
        (own,),
        (rows, prop_phase.T, amplitude[0].T, probe_field),
        (rows_shape,),
    )
    gathered = exchange(packed, "col")
    grads = call(
        main_kernel,
        piece_shape,
        (own, me),
        (gathered, jnp.asarray(dft_tables())),
        ((4, *halves), (2, *halves), (N, N), (2, *halves), (2, *halves), (2, *halves), rows_shape),
    )
    returned = exchange(grads, "pos_1")
    summed = call(gather_kernel, (Y * C, TILE, LANES), (line_offsets, me), (returned,), (strip_shape,))
    tiles = exchange(summed, ("pos_0", "col"))
    return call(merge_kernel, (2, 2, TILE, C * CLASS_IN_STRIP), (), (tiles, jnp.asarray(order.T)))


def solution(mesh):
    finer = Mesh(mesh.devices.reshape(Y, Z, C), ("pos_0", "pos_1", "col"))
    return jax.shard_map(
        per_device,
        mesh=finer,
        in_specs=(
            P(None, None, POS, "col"),
            P(None, "col", None),
            P(None, "col"),
            P(POS, None, "col"),
            P(POS, None),
            P(POS),
        ),
        out_specs=P(None, None, POS, "col"),
        check_vma=False,
    )
```

```python
import jax
import jax.numpy as jnp
import numpy as np
from jax import lax
from jax.experimental import pallas as pl
from jax.experimental.pallas import tpu as pltpu
from jax.sharding import Mesh
from jax.sharding import PartitionSpec as P

POS = ("pos_0", "pos_1")
MOD_FLOOR = 0.1

Y, Z, C = 8, 12, 8
CHIPS, CORES = 4, 2
N = 256
PLANES = 4
TILE = 8
CLASS_IN_STRIP = 12
CLASS_IN_PATCH = 32
TILES_PER_Z = 3
LANES = 128
F32 = jnp.float32
BF16 = jnp.bfloat16


def exchange(x, axes):
    return lax.all_to_all(x, axes, 0, 0, tiled=True)


def class_order():
    table = np.zeros((C * CLASS_IN_STRIP, LANES), np.float32)
    for j in range(C):
        for u in range(CLASS_IN_STRIP):
            table[C * u + j, 16 * j + u] = 1.0
    return table


def dft_tables():
    counter = np.arange(N)
    angle = (counter[:, None] * counter[None, :] % N) * (2.0 * np.pi / N)
    cosine, sine = np.cos(angle) / 16.0, np.sin(angle) / 16.0
    parts = []
    for table in (cosine, cosine + sine, cosine - sine):
        table = table.astype(np.float32)
        high = table.astype(jnp.bfloat16)
        low = (table - high.astype(np.float32)).astype(jnp.bfloat16)
        parts += [high, low]
    return np.stack(parts)


def lanes():
    return lax.broadcasted_iota(jnp.int32, (TILE, LANES), 1)


def between(lane, low, width):
    return (lane >= low) & (lane < low + width)


def rolled(x, shift):
    if isinstance(shift, int):
        shift = shift % LANES
        return pltpu.roll(x, shift, 1) if shift else x
    return pltpu.roll(x, (shift + 2 * LANES) & (LANES - 1), 1)


def spread_masks(shift):
    lane = lanes()
    row = lax.broadcasted_iota(jnp.int32, (TILE, LANES), 0)
    base = lane - jnp.where(row < 4, 0, 16) - shift + 4 * LANES
    return [((base - 32 * p) & (LANES - 1)) < CLASS_IN_STRIP for p in range(PLANES)]


def upper_half():
    return lax.broadcasted_iota(jnp.int32, (TILE, LANES), 0) < 4


def folded(piece):
    return (piece + pltpu.roll(piece, 4, 0))[:4]


def unfolded(piece):
    return jnp.concatenate([piece, piece], axis=0)


def two_shifts(x, shift, low):
    return jnp.where(low, rolled(x, shift), rolled(x, shift + 16))


def split_kernel(me_ref, x_ref, order_ref, o_ref):
    shift = CLASS_IN_STRIP * me_ref[1]
    tile = x_ref[...].reshape(PLANES * TILE, C * CLASS_IN_STRIP)
    ordered = jnp.dot(
        tile, order_ref[...], precision=lax.Precision.HIGHEST, preferred_element_type=F32
    )
    masks, low = spread_masks(shift), upper_half()
    for j in range(C):
        piece = jnp.zeros((TILE, LANES), F32)
        for p in range(PLANES):
            moved = two_shifts(ordered[p * TILE : (p + 1) * TILE], shift + 32 * p - 16 * j, low)
            piece = jnp.where(masks[p], moved, piece)
        piece = folded(piece)
        for y in range(Y):
            o_ref[y * C + j] = piece


def window(off_ref, me_ref, z):
    row, col = off_ref[z, 0, 0], off_ref[z, 0, 1]
    z_me, c_me = me_ref[0], me_ref[1]
    first = lax.shift_right_logical(row, 3)
    ahead = lax.rem(z_me - first + 6 * Z, Z)
    y_first = lax.div(first + ahead - z_me, Z)
    u_first = lax.shift_right_logical(col - c_me + 7, 3)
    return y_first, u_first


def select_kernel(off_ref, me_ref, x_ref, o_ref, strip_ref):
    lane, low = lanes(), upper_half()
    masks = [spread_masks(CLASS_IN_STRIP * j) for j in range(C)]
    for y in range(Y):
        pieces = [unfolded(x_ref[y * C + j]) for j in range(C)]
        for p in range(PLANES):
            line = pieces[0]
            for j in range(1, C):
                line = jnp.where(masks[j][p], pieces[j], line)
            strip_ref[p, y] = jnp.where(low, rolled(line, -32 * p), rolled(line, -32 * p - 16))
    for p in range(PLANES):
        strip_ref[p, Y] = jnp.zeros((TILE, LANES), F32)
    for z in range(Z):
        y_first, u_first = window(off_ref, me_ref, z)
        for k in range(TILES_PER_Z):
            piece = rolled(strip_ref[0, y_first + k], LANES - u_first)
            for p in range(1, PLANES):
                moved = rolled(strip_ref[p, y_first + k], 32 * p - u_first)
                piece = jnp.where(lane >= 32 * p, moved, piece)
            o_ref[z, k * TILE : (k + 1) * TILE] = piece


def pack_kernel(own_ref, x_ref, phase_ref, amp_ref, probe_ref, o_ref, rows_ref):
    row = own_ref[0, 0]
    first = lax.shift_right_logical(row, 3)
    for m in range(Z * TILES_PER_Z):
        k = m // Z
        rows_ref[m * TILE : (m + 1) * TILE] = x_ref[
            lax.rem(first + m, Z), k * TILE : (k + 1) * TILE
        ]
    patch = rows_ref[pl.ds(row & 7, N), :].T
    for copy in range(CHIPS):
        o_ref[copy, 0:128] = patch
        o_ref[copy, 128:160] = phase_ref[...]
        o_ref[copy, 160:192] = amp_ref[...]
        o_ref[copy, 192:224] = probe_ref[0]
        o_ref[copy, 224:256] = probe_ref[1]


def two_terms(x):
    high = x.astype(BF16)
    return high, (x - high.astype(F32)).astype(BF16)


def product(first, second):
    return jnp.dot(
        jnp.concatenate([first[0], first[0], first[1]], axis=1),
        jnp.concatenate([second[0], second[1], second[0]], axis=0),
        preferred_element_type=F32,
    )


def store(ref, at, value):
    ref[at, 0] = value[:, :LANES]
    ref[at, 1] = value[:, LANES:]


def load(ref, at, rows=slice(None)):
    return jnp.concatenate([ref[at, 0, rows, :], ref[at, 1, rows, :]], axis=1)


def main_kernel(
    own_ref, count_ref, me_ref, g_ref, other_ref, tab_ref, o_ref,
    patch_ref, h_ref, amp_ref, raw_ref, probe_ref, wave_ref, x_ref, rows_ref,
):
    row, col = own_ref[0, 0], own_ref[0, 1]
    core = me_ref[1] & 1
    for source_ref, core_of in ((g_ref, core), (other_ref, 1 - core)):
        for chip in range(CHIPS):
            j = CORES * chip + core_of
            s = (j - col + 1024) & (C - 1)
            mine = pl.ds(pl.multiple_of(32 * j, 32), 32)
            phase = source_ref[chip, 128:160, :]
            cosine, sine = jnp.cos(phase), jnp.sin(phase)
            amp_ref[mine, :] = source_ref[chip, 160:192, :]
            raw_ref[0, mine, :] = source_ref[chip, 192:224, :]
            raw_ref[1, mine, :] = source_ref[chip, 224:256, :]
            for half in range(2):
                part = slice(half * LANES, (half + 1) * LANES)
                h_ref[0, half, mine, :] = cosine[:, part]
                h_ref[1, half, mine, :] = sine[:, part]
                for p in range(PLANES):
                    patch_ref[p, half, pl.ds(s, CLASS_IN_PATCH, stride=C), :] = source_ref[
                        chip, p * 32 : (p + 1) * 32, part
                    ]
    store(probe_ref, 0, raw_ref[0].T)
    store(probe_ref, 1, raw_ref[1].T)

    def table(k):
        return tab_ref[2 * k], tab_ref[2 * k + 1]

    def held(ref, at=0, rows=slice(None)):
        return load(ref, at, rows), load(ref, at + 1, rows)

    def keep(ref, pair):
        store(ref, 0, pair[0])
        store(ref, 1, pair[1])

    def stage(pair, inverse, left):
        real_table, imag_table = (1, 2) if inverse else (2, 1)
        real, imag = pair
        both = two_terms(real + imag)
        real, imag = two_terms(real), two_terms(imag)

        def times(data, k):
            return product(table(k), data) if left else product(data, table(k))

        common = times(both, 0)
        return common - times(imag, real_table), common - times(real, imag_table)

    def transform(pair, inverse):
        keep(x_ref, stage(pair, inverse, True))
        keep(x_ref, stage(held(x_ref), inverse, False))
        return held(x_ref)

    def times(a, b):
        return a[0] * b[0] - a[1] * b[1], a[0] * b[1] + a[1] * b[0]

    def conj_times(a, b):
        return a[0] * b[0] + a[1] * b[1], a[0] * b[1] - a[1] * b[0]

    spectrum = transform(times(held(probe_ref), held(patch_ref)), False)
    wave = transform(times(held(h_ref), spectrum), True)
    keep(wave_ref, wave)
    far = transform(times(held(wave_ref), held(patch_ref, 2)), False)
    modulus = jnp.maximum(jnp.sqrt(far[0] * far[0] + far[1] * far[1]), MOD_FLOOR)
    ratio = amp_ref[...] / modulus
    back = transform((far[0] - ratio * far[0], far[1] - ratio * far[1]), True)
    keep(wave_ref, conj_times(held(wave_ref), back))
    toward = transform(conj_times(held(patch_ref, 2), back), False)
    keep(x_ref, stage(conj_times(held(h_ref), toward), True, True))
    mine = pl.ds((me_ref[1] - col + 1024) & (C - 1), CLASS_IN_PATCH, stride=C)
    back = stage(held(x_ref, 0, mine), True, False)
    first_grad = conj_times(held(probe_ref, 0, mine), back)
    second_grad = held(wave_ref, 0, mine)
    alive = (count_ref[0] > 0).astype(F32)
    grads = jnp.concatenate([*first_grad, *second_grad], axis=0) * alive
    rows_ref[...] = jnp.zeros_like(rows_ref)
    rows_ref[pl.ds(row & 7, N), :] = grads.T
    first = lax.shift_right_logical(row, 3)
    for m in range(Z * TILES_PER_Z):
        k = m // Z
        o_ref[lax.rem(first + m, Z), k * TILE : (k + 1) * TILE] = rows_ref[
            m * TILE : (m + 1) * TILE
        ]


def gather_kernel(off_ref, me_ref, x_ref, o_ref, sum_ref):
    lane = lanes()
    sum_ref[...] = jnp.zeros_like(sum_ref)
    for z in range(Z):
        y_first, u_first = window(off_ref, me_ref, z)
        inside = between(lane, u_first, CLASS_IN_PATCH)
        for k in range(TILES_PER_Z):
            piece = x_ref[z, k * TILE : (k + 1) * TILE]
            for p in range(PLANES):
                moved = jnp.where(inside, rolled(piece, u_first - 32 * p), 0.0)
                sum_ref[p, y_first + k] += moved
    masks, low = [spread_masks(CLASS_IN_STRIP * j) for j in range(C)], upper_half()
    for y in range(Y):
        lines = [two_shifts(sum_ref[p, y], 32 * p, low) for p in range(PLANES)]
        for j in range(C):
            piece = jnp.zeros((TILE, LANES), F32)
            for p in range(PLANES):
                piece = jnp.where(masks[j][p], lines[p], piece)
            o_ref[y * C + j] = folded(piece)


def merge_kernel(me_ref, x_ref, order_ref, o_ref):
    lane, low = lanes(), upper_half()
    shift = CLASS_IN_STRIP * me_ref[1]
    sums = []
    for j in range(C):
        total = x_ref[j]
        for y in range(1, Y):
            total = total + x_ref[y * C + j]
        sums.append(unfolded(total))
    planes = []
    for p in range(PLANES):
        line = jnp.zeros((TILE, LANES), F32)
        for j in range(C):
            start = 16 * j - shift - 32 * p
            moved = jnp.where(low, rolled(sums[j], start), rolled(sums[j], start - 16))
            line = jnp.where(between(lane, 16 * j, CLASS_IN_STRIP), moved, line)
        planes.append(line)
    ordered = jnp.concatenate(planes, axis=0)
    tile = jnp.dot(
        ordered, order_ref[...], precision=lax.Precision.HIGHEST, preferred_element_type=F32
    )
    o_ref[...] = tile.reshape(2, 2, TILE, C * CLASS_IN_STRIP)


IN_VMEM = pl.BlockSpec(memory_space=pltpu.VMEM)
IN_SMEM = pl.BlockSpec(memory_space=pltpu.SMEM)


def call(kernel, out_shape, scalars, arrays, scratch=(), limit=8):
    return pl.pallas_call(
        kernel,
        out_shape=jax.ShapeDtypeStruct(out_shape, F32),
        in_specs=[IN_SMEM] * len(scalars) + [IN_VMEM] * len(arrays),
        out_specs=IN_VMEM,
        scratch_shapes=[pltpu.VMEM(shape, F32) for shape in scratch],
        compiler_params=pltpu.CompilerParams(vmem_limit_bytes=limit * 1024 * 1024),
    )(*scalars, *arrays)


def per_device(object_layers, probe_field, prop_phase, amplitude, offsets, counts):
    order = class_order()
    strip_shape = (PLANES, Y + 1, TILE, LANES)
    fold_shape = (Y * C, TILE // 2, LANES)
    piece_shape = (Z, TILES_PER_Z * TILE, LANES)
    rows_shape = (Z * TILES_PER_Z * TILE + TILE, LANES)
    halves = (2, N, LANES)
    me = jnp.stack(
        [lax.axis_index("pos_1"), lax.axis_index("col_0") * CORES + lax.axis_index("col_1")]
    ).astype(jnp.int32)
    line_offsets = exchange(jnp.broadcast_to(offsets[None], (Z, 1, 2)), "pos_1")
    split = call(split_kernel, fold_shape, (me,), (object_layers, jnp.asarray(order)))
    columns = exchange(split, ("pos_0", "col_0", "col_1"))
    chosen = call(select_kernel, piece_shape, (line_offsets, me), (columns,), (strip_shape,))
    rows = exchange(chosen, "pos_1")
    packed = call(
        pack_kernel,
        (CHIPS, N, N),
        (offsets,),
        (rows, prop_phase.T, amplitude[0].T, probe_field),
        (rows_shape,),
    )
    gathered = exchange(packed, "col_0")
    other = lax.ppermute(gathered, "col_1", [(0, 1), (1, 0)])
    grads = call(
        main_kernel,
        piece_shape,
        (offsets, counts, me),
        (gathered, other, jnp.asarray(dft_tables())),
        ((4, *halves), (2, *halves), (N, N), (2, N, N), (2, *halves), (2, *halves), (2, *halves), rows_shape),
        limit=24,
    )
    returned = exchange(grads, "pos_1")
    summed = call(gather_kernel, fold_shape, (line_offsets, me), (returned,), (strip_shape,))
    tiles = exchange(summed, ("pos_0", "col_0", "col_1"))
    return call(
        merge_kernel, (2, 2, TILE, C * CLASS_IN_STRIP), (me,), (tiles, jnp.asarray(order.T))
    )


COL = ("col_0", "col_1")


def solution(mesh):
    finer = Mesh(mesh.devices.reshape(Y, Z, CHIPS, CORES), POS + COL)
    return jax.shard_map(
        per_device,
        mesh=finer,
        in_specs=(
            P(None, None, POS, COL),
            P(None, COL, None),
            P(None, COL),
            P(POS, None, COL),
            P(POS, None),
            P(POS),
        ),
        out_specs=P(None, None, POS, COL),
        check_vma=False,
    )
```

```python
import math

import jax
import jax.numpy as jnp
import numpy as np
from jax import lax
from jax.experimental import pallas as pl
from jax.experimental.pallas import tpu as pltpu
from jax.sharding import Mesh
from jax.sharding import PartitionSpec as P

POS = ("pos_0", "pos_1")
MOD_FLOOR = 0.1

Y, Z, C = 8, 12, 8
CHIPS, CORES = 4, 2
N = 256
PLANES = 4
TILE = 8
CLASS_IN_STRIP = 12
CLASS_IN_PATCH = 32
TILES_PER_Z = 3
LANES = 128
CHUNK = 32
F32 = jnp.float32
SINE_SERIES = [(-1.0) ** k / math.factorial(2 * k + 1) for k in range(6)]
COSINE_SERIES = [(-1.0) ** k / math.factorial(2 * k) for k in range(7)]
BF16 = jnp.bfloat16


def exchange(x, axes):
    return lax.all_to_all(x, axes, 0, 0, tiled=True)


def class_order(shape, column_axis):
    column = lax.broadcasted_iota(jnp.int32, shape, column_axis)
    lane = lax.broadcasted_iota(jnp.int32, shape, 1 - column_axis)
    place = (column & (C - 1)) * 16 + lax.shift_right_logical(column, 3)
    return (place == lane).astype(F32)


def dft_tables():
    counter = np.arange(N)
    angle = (counter[:, None] * counter[None, :] % N) * (2.0 * np.pi / N)
    cosine, sine = np.cos(angle) / 16.0, np.sin(angle) / 16.0
    parts = []
    for table in (cosine, cosine + sine, cosine - sine):
        table = table.astype(np.float32)
        high = table.astype(jnp.bfloat16)
        low = (table - high.astype(np.float32)).astype(jnp.bfloat16)
        parts += [high, low]
    return np.stack(parts)


def lanes():
    return lax.broadcasted_iota(jnp.int32, (TILE, LANES), 1)


def between(lane, low, width):
    return (lane >= low) & (lane < low + width)


def rolled(x, shift):
    if isinstance(shift, int):
        shift = shift % LANES
        return pltpu.roll(x, shift, 1) if shift else x
    return pltpu.roll(x, (shift + 2 * LANES) & (LANES - 1), 1)


def spread_masks(shift):
    lane = lanes()
    row = lax.broadcasted_iota(jnp.int32, (TILE, LANES), 0)
    base = lane - jnp.where(row < 4, 0, 16) - shift + 4 * LANES
    return [((base - 32 * p) & (LANES - 1)) < CLASS_IN_STRIP for p in range(PLANES)]


def upper_half():
    return lax.broadcasted_iota(jnp.int32, (TILE, LANES), 0) < 4


def folded(piece):
    return (piece + pltpu.roll(piece, 4, 0))[:4]


def unfolded(piece):
    return jnp.concatenate([piece, piece], axis=0)


def two_shifts(x, shift, low):
    return jnp.where(low, rolled(x, shift), rolled(x, shift + 16))


def split_kernel(me_ref, own_ref, x_ref, o_ref):
    shift = CLASS_IN_STRIP * me_ref[1]
    tile = x_ref[...].reshape(PLANES * TILE, C * CLASS_IN_STRIP)
    order = class_order((C * CLASS_IN_STRIP, LANES), 0)
    ordered = jnp.dot(
        tile, order, precision=lax.Precision.HIGHEST, preferred_element_type=F32
    )
    lane = lanes()
    base = lane - shift + 4 * LANES
    row, col = own_ref[0, 0].astype(F32), own_ref[0, 1].astype(F32)
    corner = jnp.where((base & (LANES - 1)) == CLASS_IN_STRIP, row, 0.0)
    corner = jnp.where((base & (LANES - 1)) == CLASS_IN_STRIP + 1, col, corner)
    for j in range(C):
        piece = corner
        for p in range(PLANES):
            moved = rolled(ordered[p * TILE : (p + 1) * TILE], shift + 32 * p - 16 * j)
            piece = jnp.where(((base - 32 * p) & (LANES - 1)) < CLASS_IN_STRIP, moved, piece)
        o_ref[j * TILE : (j + 1) * TILE] = piece


def widen_kernel(own_ref, x_ref, o_ref):
    lane = lanes()
    row, col = own_ref[0, 0].astype(F32), own_ref[0, 1].astype(F32)
    for p in range(PLANES):
        line = x_ref[0:TILE]
        for j in range(1, C):
            inside = ((lane - CLASS_IN_STRIP * j - 32 * p + 2 * LANES) & (LANES - 1)) < CLASS_IN_STRIP
            line = jnp.where(inside, x_ref[j * TILE : (j + 1) * TILE], line)
        line = rolled(line, -32 * p)
        line = jnp.where(lane == C * CLASS_IN_STRIP, row, line)
        line = jnp.where(lane == C * CLASS_IN_STRIP + 1, col, line)
        for z in range(Z):
            o_ref[z, p * TILE : (p + 1) * TILE] = line


def window(off_ref, me_ref, z):
    row, col = off_ref[z, 0], off_ref[z, 1]
    z_me, c_me = me_ref[0], me_ref[1]
    first = lax.shift_right_logical(row, 3)
    ahead = lax.rem(z_me - first + 6 * Z, Z)
    y_first = lax.div(first + ahead - z_me, Z)
    u_first = lax.shift_right_logical(col - c_me + 7, 3)
    return y_first, u_first


def select_kernel(off_ref, me_ref, x_ref, o_ref, strip_ref):
    lane = lax.broadcasted_iota(jnp.int32, (CLASS_IN_PATCH, LANES), 1)
    for p in range(PLANES):
        for z in range(Z):
            strip_ref[p, pl.ds(z, Y, stride=Z), :] = x_ref[z, p * TILE : (p + 1) * TILE]
    for y in range(Y):
        n_first = lax.shift_right_logical(off_ref[y, 0] - me_ref[2] + 7, 3)
        u_first = lax.shift_right_logical(off_ref[y, 1] - me_ref[1] + 7, 3)
        rows = pl.ds(n_first, CLASS_IN_PATCH)
        piece = rolled(strip_ref[0, rows, :], LANES - u_first)
        for p in range(1, PLANES):
            moved = rolled(strip_ref[p, rows, :], 32 * p - u_first)
            piece = jnp.where(lane >= 32 * p, moved, piece)
        o_ref[y] = piece


def pack_kernel(own_ref, x_ref, phase_ref, amp_ref, probe_ref, o_ref, rows_ref):
    row = own_ref[0, 0]
    for s in range(Y):
        rows_ref[pl.ds(s, CLASS_IN_PATCH, stride=Y), :] = x_ref[(row + s) & (Y - 1)]
    patch = rows_ref[...].T
    for copy in range(CHIPS):
        o_ref[copy, 0:128] = patch
        o_ref[copy, 128:160] = phase_ref[...]
        o_ref[copy, 160:192] = amp_ref[...]
        o_ref[copy, 192:224] = probe_ref[0]
        o_ref[copy, 224:256] = probe_ref[1]


def two_terms(x):
    high = x.astype(BF16)
    return high, (x - high.astype(F32)).astype(BF16)


def product(first, second):
    return jnp.dot(
        jnp.concatenate([first[0], first[0], first[1]], axis=1),
        jnp.concatenate([second[0], second[1], second[0]], axis=0),
        preferred_element_type=F32,
    )


def cosine_and_sine(angle):
    half = 0.5 * angle
    square = half * half
    sine = jnp.full_like(square, SINE_SERIES[-1])
    for coefficient in SINE_SERIES[-2::-1]:
        sine = sine * square + coefficient
    cosine = jnp.full_like(square, COSINE_SERIES[-1])
    for coefficient in COSINE_SERIES[-2::-1]:
        cosine = cosine * square + coefficient
    sine = sine * half
    twice = sine + sine
    return 1.0 - twice * sine, twice * cosine


def store(ref, at, value):
    ref[at, 0] = value[:, :LANES]
    ref[at, 1] = value[:, LANES:]


def load(ref, at, rows=slice(None)):
    return jnp.concatenate([ref[at, 0, rows, :], ref[at, 1, rows, :]], axis=1)


def main_kernel(
    own_ref, count_ref, me_ref, g_ref, other_ref, tab_ref, o_ref,
    patch_ref, h_ref, amp_ref, raw_ref, probe_ref, wave_ref, x_ref, rows_ref, op_ref,
):
    row, col = own_ref[0, 0], own_ref[0, 1]
    core = me_ref[1] & 1
    for source_ref, core_of in ((g_ref, core), (other_ref, 1 - core)):
        for chip in range(CHIPS):
            j = CORES * chip + core_of
            s = (j - col + 1024) & (C - 1)
            mine = pl.ds(pl.multiple_of(32 * j, 32), 32)
            amp_ref[mine, :] = source_ref[chip, 160:192, :]
            raw_ref[0, mine, :] = source_ref[chip, 192:224, :]
            raw_ref[1, mine, :] = source_ref[chip, 224:256, :]
            for half in range(2):
                part = slice(half * LANES, (half + 1) * LANES)
                for p in range(PLANES):
                    patch_ref[p, half, pl.ds(s, CLASS_IN_PATCH, stride=C), :] = source_ref[
                        chip, p * 32 : (p + 1) * 32, part
                    ]
    store(probe_ref, 0, raw_ref[0].T)
    store(probe_ref, 1, raw_ref[1].T)

    def table(k):
        return tab_ref[2 * k], tab_ref[2 * k + 1]

    def held(ref, at=0, rows=slice(None)):
        return load(ref, at, rows), load(ref, at + 1, rows)

    def keep(ref, pair):
        store(ref, 0, pair[0])
        store(ref, 1, pair[1])

    def keep_rows(ref, rows, pair):
        for at in range(2):
            ref[at, 0, rows] = pair[at][:, :LANES]
            ref[at, 1, rows] = pair[at][:, LANES:]

    def stage(inverse, left, rows=N):
        real_table, imag_table = (1, 2) if inverse else (2, 1)

        def times(at, k):
            data = (op_ref[at, :rows], op_ref[at + 1, :rows])
            return product(table(k), data) if left else product(data, table(k))

        common = times(0, 0)
        return common - times(4, real_table), common - times(2, imag_table)

    def prepare(rows, pair):
        real, imag = pair
        for at, part in ((0, real + imag), (2, real), (4, imag)):
            op_ref[at, rows], op_ref[at + 1, rows] = two_terms(part)

    def chunks(step):
        for start in range(0, N, CHUNK):
            step(slice(start, start + CHUNK))

    def propagator():
        for source_ref, core_of in ((g_ref, core), (other_ref, 1 - core)):
            for chip in range(CHIPS):
                rows = pl.ds(pl.multiple_of(32 * (CORES * chip + core_of), 32), 32)
                keep_rows(h_ref, rows, cosine_and_sine(source_ref[chip, 128:160, :]))

    def transform(inverse, meanwhile=None):
        keep(x_ref, stage(inverse, True))
        if meanwhile:
            meanwhile()
        chunks(lambda rows: prepare(rows, held(x_ref, 0, rows)))
        keep(x_ref, stage(inverse, False))

    def times(a, b):
        return a[0] * b[0] - a[1] * b[1], a[0] * b[1] + a[1] * b[0]

    def conj_times(a, b):
        return a[0] * b[0] + a[1] * b[1], a[0] * b[1] - a[1] * b[0]

    def enter(rows):
        prepare(rows, times(held(probe_ref, 0, rows), held(patch_ref, 0, rows)))

    def propagate(rows):
        prepare(rows, times(held(h_ref, 0, rows), held(x_ref, 0, rows)))

    def modulate(rows):
        wave = held(x_ref, 0, rows)
        keep_rows(wave_ref, rows, wave)
        prepare(rows, times(wave, held(patch_ref, 2, rows)))

    def correct(rows):
        real, imag = held(x_ref, 0, rows)
        modulus = jnp.maximum(jnp.sqrt(real * real + imag * imag), MOD_FLOOR)
        ratio = amp_ref[rows] / modulus
        prepare(rows, (real - ratio * real, imag - ratio * imag))

    def turn_back(rows):
        back = held(x_ref, 0, rows)
        keep_rows(wave_ref, rows, conj_times(held(wave_ref, 0, rows), back))
        prepare(rows, conj_times(held(patch_ref, 2, rows), back))

    def propagate_back(rows):
        prepare(rows, conj_times(held(h_ref, 0, rows), held(x_ref, 0, rows)))

    chunks(enter)
    transform(False, propagator)
    chunks(propagate)
    transform(True)
    chunks(modulate)
    transform(False)
    chunks(correct)
    transform(True)
    chunks(turn_back)
    transform(False)
    chunks(propagate_back)
    keep(x_ref, stage(True, True))
    mine = pl.ds((me_ref[1] - col + 1024) & (C - 1), CLASS_IN_PATCH, stride=C)
    prepare(slice(0, CLASS_IN_PATCH), held(x_ref, 0, mine))
    back = stage(True, False, CLASS_IN_PATCH)
    first_grad = conj_times(held(probe_ref, 0, mine), back)
    second_grad = held(wave_ref, 0, mine)
    alive = (count_ref[0] > 0).astype(F32)
    grads = jnp.concatenate([*first_grad, *second_grad], axis=0) * alive
    rows_ref[...] = jnp.zeros_like(rows_ref)
    rows_ref[pl.ds(row & 7, N), :] = grads.T
    first = lax.shift_right_logical(row, 3)
    for m in range(Z * TILES_PER_Z):
        k = m // Z
        o_ref[lax.rem(first + m, Z), k * TILE : (k + 1) * TILE] = rows_ref[
            m * TILE : (m + 1) * TILE
        ]


def gather_kernel(off_ref, me_ref, x_ref, o_ref, sum_ref):
    lane = lanes()
    sum_ref[...] = jnp.zeros_like(sum_ref)
    for z in range(Z):
        y_first, u_first = window(off_ref, me_ref, z)
        inside = between(lane, u_first, CLASS_IN_PATCH)
        for k in range(TILES_PER_Z):
            piece = x_ref[z, k * TILE : (k + 1) * TILE]
            for p in range(PLANES):
                moved = jnp.where(inside, rolled(piece, u_first - 32 * p), 0.0)
                sum_ref[p, y_first + k] += moved
    masks, low = [spread_masks(CLASS_IN_STRIP * j) for j in range(C)], upper_half()
    for y in range(Y):
        lines = [two_shifts(sum_ref[p, y], 32 * p, low) for p in range(PLANES)]
        for j in range(C):
            piece = jnp.zeros((TILE, LANES), F32)
            for p in range(PLANES):
                piece = jnp.where(masks[j][p], lines[p], piece)
            o_ref[y * C + j] = folded(piece)


def merge_kernel(me_ref, x_ref, o_ref):
    lane, low = lanes(), upper_half()
    shift = CLASS_IN_STRIP * me_ref[1]
    sums = []
    for j in range(C):
        total = x_ref[j]
        for y in range(1, Y):
            total = total + x_ref[y * C + j]
        sums.append(unfolded(total))
    planes = []
    for p in range(PLANES):
        line = jnp.zeros((TILE, LANES), F32)
        for j in range(C):
            start = 16 * j - shift - 32 * p
            moved = jnp.where(low, rolled(sums[j], start), rolled(sums[j], start - 16))
            line = jnp.where(between(lane, 16 * j, CLASS_IN_STRIP), moved, line)
        planes.append(line)
    ordered = jnp.concatenate(planes, axis=0)
    order = class_order((LANES, C * CLASS_IN_STRIP), 1)
    tile = jnp.dot(
        ordered, order, precision=lax.Precision.HIGHEST, preferred_element_type=F32
    )
    o_ref[...] = tile.reshape(2, 2, TILE, C * CLASS_IN_STRIP)


IN_VMEM = pl.BlockSpec(memory_space=pltpu.VMEM)
IN_SMEM = pl.BlockSpec(memory_space=pltpu.SMEM)


def call(kernel, out_shape, scalars, arrays, scratch=(), limit=8, extra=()):
    return pl.pallas_call(
        kernel,
        out_shape=jax.ShapeDtypeStruct(out_shape, F32),
        in_specs=[IN_SMEM] * len(scalars) + [IN_VMEM] * len(arrays),
        out_specs=IN_VMEM,
        scratch_shapes=[pltpu.VMEM(shape, F32) for shape in scratch] + list(extra),
        compiler_params=pltpu.CompilerParams(vmem_limit_bytes=limit * 1024 * 1024),
    )(*scalars, *arrays)


def per_device(object_layers, probe_field, prop_phase, amplitude, offsets, counts):
    strip_shape = (PLANES, Y + 1, TILE, LANES)
    fold_shape = (Y * C, TILE // 2, LANES)
    piece_shape = (Z, TILES_PER_Z * TILE, LANES)
    rows_shape = (Z * TILES_PER_Z * TILE + TILE, LANES)
    halves = (2, N, LANES)
    col_at = lax.axis_index("col_0") * CORES + lax.axis_index("col_1")
    me = jnp.stack([lax.axis_index("pos_1"), col_at, lax.axis_index("pos_0")]).astype(jnp.int32)
    split = call(split_kernel, (C * TILE, LANES), (me, offsets), (object_layers,))
    lines = exchange(split.reshape(C * Y, 1, LANES), COL + ("pos_0",)).reshape(C * Y, LANES)
    y_offsets = lines[:Y, CLASS_IN_STRIP : CLASS_IN_STRIP + 2].astype(jnp.int32)
    wide = call(widen_kernel, (Z, PLANES * TILE, LANES), (offsets,), (lines,))
    blocks = exchange(wide, "pos_1")
    width = C * CLASS_IN_STRIP
    z_offsets = blocks[:, 0, width : width + 2].astype(jnp.int32)
    chosen = call(
        select_kernel,
        (Y, CLASS_IN_PATCH, LANES),
        (y_offsets, me),
        (blocks,),
        ((PLANES, Y * Z, LANES),),
    )
    rows = exchange(chosen, "pos_0")
    packed = call(
        pack_kernel,
        (CHIPS, N, N),
        (offsets,),
        (rows, prop_phase.T, amplitude[0].T, probe_field),
        ((N, LANES),),
    )
    gathered = exchange(packed, "col_0")
    other = lax.ppermute(gathered, "col_1", [(0, 1), (1, 0)])
    grads = call(
        main_kernel,
        piece_shape,
        (offsets, counts, me),
        (gathered, other, jnp.asarray(dft_tables())),
        ((4, *halves), (2, *halves), (N, N), (2, N, N), (2, *halves), (2, *halves), (2, *halves), rows_shape),
        limit=24,
        extra=[pltpu.VMEM((6, N, N), BF16)],
    )
    returned = exchange(grads, "pos_1")
    summed = call(gather_kernel, fold_shape, (z_offsets, me), (returned,), (strip_shape,))
    tiles = exchange(summed, ("pos_0", "col_0", "col_1"))
    return call(
        merge_kernel, (2, 2, TILE, C * CLASS_IN_STRIP), (me,), (tiles,)
    )


COL = ("col_0", "col_1")


def solution(mesh):
    finer = Mesh(mesh.devices.reshape(Y, Z, CHIPS, CORES), POS + COL)
    return jax.shard_map(
        per_device,
        mesh=finer,
        in_specs=(
            P(None, None, POS, COL),
            P(None, COL, None),
            P(None, COL),
            P(POS, None, COL),
            P(POS, None),
            P(POS),
        ),
        out_specs=P(None, None, POS, COL),
        check_vma=False,
    )
```

```python
import math

import jax
import jax.numpy as jnp
import numpy as np
from jax import lax
from jax.experimental import pallas as pl
from jax.experimental.pallas import tpu as pltpu
from jax.sharding import Mesh
from jax.sharding import PartitionSpec as P

POS = ("pos_0", "pos_1")
MOD_FLOOR = 0.1

Y, Z, C = 8, 12, 8
CHIPS, CORES = 4, 2
N = 256
PLANES = 4
TILE = 8
CLASS_IN_STRIP = 12
STRIP = C * CLASS_IN_STRIP
PIECE = 26
CLASS_IN_PATCH = 32
TILES_PER_Z = 3
LANES = 128
CHUNK = 32
F32 = jnp.float32
SINE_SERIES = [(-1.0) ** k / math.factorial(2 * k + 1) for k in range(6)]
COSINE_SERIES = [(-1.0) ** k / math.factorial(2 * k) for k in range(7)]
BF16 = jnp.bfloat16


def exchange(x, axes):
    return lax.all_to_all(x, axes, 0, 0, tiled=True)


def class_order(shape, column_axis):
    column = lax.broadcasted_iota(jnp.int32, shape, column_axis)
    lane = lax.broadcasted_iota(jnp.int32, shape, 1 - column_axis)
    place = (column & (C - 1)) * 16 + lax.shift_right_logical(column, 3)
    return (place == lane).astype(F32)


def dft_tables():
    counter = np.arange(N)
    angle = (counter[:, None] * counter[None, :] % N) * (2.0 * np.pi / N)
    cosine, sine = np.cos(angle) / 16.0, np.sin(angle) / 16.0
    parts = []
    for table in (cosine, cosine + sine, cosine - sine):
        table = table.astype(np.float32)
        high = table.astype(jnp.bfloat16)
        low = (table - high.astype(np.float32)).astype(jnp.bfloat16)
        parts += [high, low]
    return np.stack(parts)


def lanes():
    return lax.broadcasted_iota(jnp.int32, (TILE, LANES), 1)


def between(lane, low, width):
    return (lane >= low) & (lane < low + width)


def rolled(x, shift):
    if isinstance(shift, int):
        shift = shift % LANES
        return pltpu.roll(x, shift, 1) if shift else x
    return pltpu.roll(x, (shift + 2 * LANES) & (LANES - 1), 1)


def spread_masks(shift):
    lane = lanes()
    row = lax.broadcasted_iota(jnp.int32, (TILE, LANES), 0)
    base = lane - jnp.where(row < 4, 0, 16) - shift + 4 * LANES
    return [((base - 32 * p) & (LANES - 1)) < CLASS_IN_STRIP for p in range(PLANES)]


def upper_half():
    return lax.broadcasted_iota(jnp.int32, (TILE, LANES), 0) < 4


def folded(piece):
    return (piece + pltpu.roll(piece, 4, 0))[:4]


def unfolded(piece):
    return jnp.concatenate([piece, piece], axis=0)


def two_shifts(x, shift, low):
    return jnp.where(low, rolled(x, shift), rolled(x, shift + 16))


def split_kernel(me_ref, own_ref, x_ref, o_ref):
    shift = CLASS_IN_STRIP * me_ref[1]
    tile = x_ref[...].reshape(PLANES * TILE, C * CLASS_IN_STRIP)
    order = class_order((C * CLASS_IN_STRIP, LANES), 0)
    ordered = jnp.dot(
        tile, order, precision=lax.Precision.HIGHEST, preferred_element_type=F32
    )
    lane = lanes()
    base = lane - shift + 4 * LANES
    row, col = own_ref[0, 0].astype(F32), own_ref[0, 1].astype(F32)
    corner = jnp.where((base & (LANES - 1)) == CLASS_IN_STRIP, row, 0.0)
    corner = jnp.where((base & (LANES - 1)) == CLASS_IN_STRIP + 1, col, corner)
    for j in range(C):
        piece = corner
        for p in range(PLANES):
            moved = rolled(ordered[p * TILE : (p + 1) * TILE], shift + 32 * p - 16 * j)
            piece = jnp.where(((base - 32 * p) & (LANES - 1)) < CLASS_IN_STRIP, moved, piece)
        o_ref[j * TILE : (j + 1) * TILE] = piece


def widen_kernel(own_ref, x_ref, o_ref, off_ref):
    lane = lanes()
    planes = []
    for p in range(PLANES):
        line = x_ref[0:TILE]
        for j in range(1, C):
            inside = ((lane - CLASS_IN_STRIP * j - 32 * p + 2 * LANES) & (LANES - 1)) < CLASS_IN_STRIP
            line = jnp.where(inside, x_ref[j * TILE : (j + 1) * TILE], line)
        planes.append(rolled(line, -32 * p))
    packed = [
        jnp.where(lane < STRIP, planes[q], rolled(planes[3], STRIP - 32 * q)) for q in range(3)
    ]
    row, col = own_ref[0, 0].astype(F32), own_ref[0, 1].astype(F32)
    corner = jnp.where(lane[: PIECE - 3 * TILE] == 0, row, col)
    for z in range(Z):
        for q in range(3):
            o_ref[z * PIECE + q * TILE : z * PIECE + (q + 1) * TILE] = packed[q]
        o_ref[z * PIECE + 3 * TILE : (z + 1) * PIECE] = corner
    off_ref[...] = x_ref[0:TILE].astype(jnp.int32)


def window(off_ref, me_ref, z):
    row, col = off_ref[z, 0], off_ref[z, 1]
    z_me, c_me = me_ref[0], me_ref[1]
    first = lax.shift_right_logical(row, 3)
    ahead = lax.rem(z_me - first + 6 * Z, Z)
    y_first = lax.div(first + ahead - z_me, Z)
    u_first = lax.shift_right_logical(col - c_me + 7, 3)
    return y_first, u_first


def select_kernel(off_ref, me_ref, x_ref, o_ref, z_off_ref, strip_ref):
    lane = lanes()
    for z in range(Z):
        packed = [x_ref[z * PIECE + q * TILE : z * PIECE + (q + 1) * TILE] for q in range(3)]
        last = rolled(packed[2], 64 - STRIP)
        last = jnp.where(lane < 64, rolled(packed[1], 32 - STRIP), last)
        last = jnp.where(lane < 32, rolled(packed[0], -STRIP), last)
        for p, line in enumerate(packed + [last]):
            strip_ref[p, pl.ds(z, Y, stride=Z), :] = line
        z_off_ref[z : z + 1] = x_ref[z * PIECE + 3 * TILE : z * PIECE + 3 * TILE + 1].astype(jnp.int32)
    lane = lax.broadcasted_iota(jnp.int32, (CLASS_IN_PATCH, LANES), 1)
    for y in range(Y):
        row, col = off_ref[y, CLASS_IN_STRIP], off_ref[y, CLASS_IN_STRIP + 1]
        n_first = lax.shift_right_logical(row - me_ref[2] + 7, 3)
        u_first = lax.shift_right_logical(col - me_ref[1] + 7, 3)
        rows = pl.ds(n_first, CLASS_IN_PATCH)
        piece = rolled(strip_ref[0, rows, :], LANES - u_first)
        for p in range(1, PLANES):
            moved = rolled(strip_ref[p, rows, :], 32 * p - u_first)
            piece = jnp.where(lane >= 32 * p, moved, piece)
        o_ref[y] = piece


def pack_kernel(own_ref, x_ref, phase_ref, amp_ref, probe_ref, o_ref, rows_ref):
    row = own_ref[0, 0]
    for s in range(Y):
        rows_ref[pl.ds(s, CLASS_IN_PATCH, stride=Y), :] = x_ref[(row + s) & (Y - 1)]
    patch = rows_ref[...].T
    for copy in range(CHIPS):
        o_ref[copy, 0:128] = patch
        o_ref[copy, 128:160] = phase_ref[...]
        o_ref[copy, 160:192] = amp_ref[...]
        o_ref[copy, 192:224] = probe_ref[0]
        o_ref[copy, 224:256] = probe_ref[1]


def two_terms(x):
    high = x.astype(BF16)
    return high, (x - high.astype(F32)).astype(BF16)


def product(first, second):
    return jnp.dot(
        jnp.concatenate([first[0], first[0], first[1]], axis=1),
        jnp.concatenate([second[0], second[1], second[0]], axis=0),
        preferred_element_type=F32,
    )


def cosine_and_sine(angle):
    half = 0.5 * angle
    square = half * half
    sine = jnp.full_like(square, SINE_SERIES[-1])
    for coefficient in SINE_SERIES[-2::-1]:
        sine = sine * square + coefficient
    cosine = jnp.full_like(square, COSINE_SERIES[-1])
    for coefficient in COSINE_SERIES[-2::-1]:
        cosine = cosine * square + coefficient
    sine = sine * half
    twice = sine + sine
    return 1.0 - twice * sine, twice * cosine


def store(ref, at, value):
    ref[at, 0] = value[:, :LANES]
    ref[at, 1] = value[:, LANES:]


def load(ref, at, rows=slice(None)):
    return jnp.concatenate([ref[at, 0, rows, :], ref[at, 1, rows, :]], axis=1)


def main_kernel(
    own_ref, count_ref, me_ref, g_ref, other_ref, tab_ref, o_ref,
    patch_ref, h_ref, amp_ref, raw_ref, probe_ref, wave_ref, x_ref, rows_ref, op_ref,
):
    row, col = own_ref[0, 0], own_ref[0, 1]
    core = me_ref[1] & 1
    for source_ref, core_of in ((g_ref, core), (other_ref, 1 - core)):
        for chip in range(CHIPS):
            j = CORES * chip + core_of
            s = (j - col + 1024) & (C - 1)
            mine = pl.ds(pl.multiple_of(32 * j, 32), 32)
            amp_ref[mine, :] = source_ref[chip, 160:192, :]
            raw_ref[0, mine, :] = source_ref[chip, 192:224, :]
            raw_ref[1, mine, :] = source_ref[chip, 224:256, :]
            for half in range(2):
                part = slice(half * LANES, (half + 1) * LANES)
                for p in range(PLANES):
                    patch_ref[p, half, pl.ds(s, CLASS_IN_PATCH, stride=C), :] = source_ref[
                        chip, p * 32 : (p + 1) * 32, part
                    ]
    store(probe_ref, 0, raw_ref[0].T)
    store(probe_ref, 1, raw_ref[1].T)

    def table(k):
        return tab_ref[2 * k], tab_ref[2 * k + 1]

    def held(ref, at=0, rows=slice(None)):
        return load(ref, at, rows), load(ref, at + 1, rows)

    def keep(ref, pair):
        store(ref, 0, pair[0])
        store(ref, 1, pair[1])

    def keep_rows(ref, rows, pair):
        for at in range(2):
            ref[at, 0, rows] = pair[at][:, :LANES]
            ref[at, 1, rows] = pair[at][:, LANES:]

    def stage(inverse, left, rows=N):
        real_table, imag_table = (1, 2) if inverse else (2, 1)

        def times(at, k):
            data = (op_ref[at, :rows], op_ref[at + 1, :rows])
            return product(table(k), data) if left else product(data, table(k))

        common = times(0, 0)
        return common - times(4, real_table), common - times(2, imag_table)

    def prepare(rows, pair):
        real, imag = pair
        for at, part in ((0, real + imag), (2, real), (4, imag)):
            op_ref[at, rows], op_ref[at + 1, rows] = two_terms(part)

    def chunks(step):
        for start in range(0, N, CHUNK):
            step(slice(start, start + CHUNK))

    def propagator():
        for source_ref, core_of in ((g_ref, core), (other_ref, 1 - core)):
            for chip in range(CHIPS):
                rows = pl.ds(pl.multiple_of(32 * (CORES * chip + core_of), 32), 32)
                keep_rows(h_ref, rows, cosine_and_sine(source_ref[chip, 128:160, :]))

    def transform(inverse, meanwhile=None):
        keep(x_ref, stage(inverse, True))
        if meanwhile:
            meanwhile()
        chunks(lambda rows: prepare(rows, held(x_ref, 0, rows)))
        keep(x_ref, stage(inverse, False))

    def times(a, b):
        return a[0] * b[0] - a[1] * b[1], a[0] * b[1] + a[1] * b[0]

    def conj_times(a, b):
        return a[0] * b[0] + a[1] * b[1], a[0] * b[1] - a[1] * b[0]

    def enter(rows):
        prepare(rows, times(held(probe_ref, 0, rows), held(patch_ref, 0, rows)))

    def propagate(rows):
        prepare(rows, times(held(h_ref, 0, rows), held(x_ref, 0, rows)))

    def modulate(rows):
        wave = held(x_ref, 0, rows)
        keep_rows(wave_ref, rows, wave)
        prepare(rows, times(wave, held(patch_ref, 2, rows)))

    def correct(rows):
        real, imag = held(x_ref, 0, rows)
        modulus = jnp.maximum(jnp.sqrt(real * real + imag * imag), MOD_FLOOR)
        ratio = amp_ref[rows] / modulus
        prepare(rows, (real - ratio * real, imag - ratio * imag))

    def turn_back(rows):
        back = held(x_ref, 0, rows)
        keep_rows(wave_ref, rows, conj_times(held(wave_ref, 0, rows), back))
        prepare(rows, conj_times(held(patch_ref, 2, rows), back))

    def propagate_back(rows):
        prepare(rows, conj_times(held(h_ref, 0, rows), held(x_ref, 0, rows)))

    chunks(enter)
    transform(False, propagator)
    chunks(propagate)
    transform(True)
    chunks(modulate)
    transform(False)
    chunks(correct)
    transform(True)
    chunks(turn_back)
    transform(False)
    chunks(propagate_back)
    keep(x_ref, stage(True, True))
    mine = pl.ds((me_ref[1] - col + 1024) & (C - 1), CLASS_IN_PATCH, stride=C)
    prepare(slice(0, CLASS_IN_PATCH), held(x_ref, 0, mine))
    back = stage(True, False, CLASS_IN_PATCH)
    first_grad = conj_times(held(probe_ref, 0, mine), back)
    second_grad = held(wave_ref, 0, mine)
    alive = (count_ref[0] > 0).astype(F32)
    grads = jnp.concatenate([*first_grad, *second_grad], axis=0) * alive
    rows_ref[...] = jnp.zeros_like(rows_ref)
    rows_ref[pl.ds(row & 7, N), :] = grads.T
    first = lax.shift_right_logical(row, 3)
    for m in range(Z * TILES_PER_Z):
        k = m // Z
        o_ref[lax.rem(first + m, Z), k * TILE : (k + 1) * TILE] = rows_ref[
            m * TILE : (m + 1) * TILE
        ]


def gather_kernel(off_ref, me_ref, x_ref, o_ref, sum_ref):
    lane = lanes()
    sum_ref[...] = jnp.zeros_like(sum_ref)
    for z in range(Z):
        y_first, u_first = window(off_ref, me_ref, z)
        inside = between(lane, u_first, CLASS_IN_PATCH)
        for k in range(TILES_PER_Z):
            piece = x_ref[z, k * TILE : (k + 1) * TILE]
            for p in range(PLANES):
                moved = jnp.where(inside, rolled(piece, u_first - 32 * p), 0.0)
                sum_ref[p, y_first + k] += moved
    masks, low = [spread_masks(CLASS_IN_STRIP * j) for j in range(C)], upper_half()
    for y in range(Y):
        lines = [two_shifts(sum_ref[p, y], 32 * p, low) for p in range(PLANES)]
        for j in range(C):
            piece = jnp.zeros((TILE, LANES), F32)
            for p in range(PLANES):
                piece = jnp.where(masks[j][p], lines[p], piece)
            o_ref[y * C + j] = folded(piece)


def merge_kernel(me_ref, x_ref, o_ref):
    lane, low = lanes(), upper_half()
    shift = CLASS_IN_STRIP * me_ref[1]
    sums = []
    for j in range(C):
        total = x_ref[j]
        for y in range(1, Y):
            total = total + x_ref[y * C + j]
        sums.append(unfolded(total))
    planes = []
    for p in range(PLANES):
        line = jnp.zeros((TILE, LANES), F32)
        for j in range(C):
            start = 16 * j - shift - 32 * p
            moved = jnp.where(low, rolled(sums[j], start), rolled(sums[j], start - 16))
            line = jnp.where(between(lane, 16 * j, CLASS_IN_STRIP), moved, line)
        planes.append(line)
    ordered = jnp.concatenate(planes, axis=0)
    order = class_order((LANES, C * CLASS_IN_STRIP), 1)
    tile = jnp.dot(
        ordered, order, precision=lax.Precision.HIGHEST, preferred_element_type=F32
    )
    o_ref[...] = tile.reshape(2, 2, TILE, C * CLASS_IN_STRIP)


IN_VMEM = pl.BlockSpec(memory_space=pltpu.VMEM)
IN_SMEM = pl.BlockSpec(memory_space=pltpu.SMEM)


def call(kernel, out_shape, scalars, arrays, scratch=(), limit=8, extra=()):
    single = isinstance(out_shape, tuple)
    outs = [jax.ShapeDtypeStruct(*out) for out in ([(out_shape, F32)] if single else out_shape)]
    return pl.pallas_call(
        kernel,
        out_shape=outs[0] if single else outs,
        in_specs=[IN_SMEM] * len(scalars) + [IN_VMEM] * len(arrays),
        out_specs=IN_VMEM if single else [IN_VMEM] * len(outs),
        scratch_shapes=[pltpu.VMEM(shape, F32) for shape in scratch] + list(extra),
        compiler_params=pltpu.CompilerParams(vmem_limit_bytes=limit * 1024 * 1024),
    )(*scalars, *arrays)


def per_device(object_layers, probe_field, prop_phase, amplitude, offsets, counts):
    strip_shape = (PLANES, Y + 1, TILE, LANES)
    fold_shape = (Y * C, TILE // 2, LANES)
    piece_shape = (Z, TILES_PER_Z * TILE, LANES)
    rows_shape = (Z * TILES_PER_Z * TILE + TILE, LANES)
    halves = (2, N, LANES)
    col_at = lax.axis_index("col_0") * CORES + lax.axis_index("col_1")
    me = jnp.stack([lax.axis_index("pos_1"), col_at, lax.axis_index("pos_0")]).astype(jnp.int32)
    split = call(split_kernel, (C * TILE, LANES), (me, offsets), (object_layers,))
    lines = exchange(split.reshape(C * Y, 1, LANES), COL + ("pos_0",)).reshape(C * Y, LANES)
    wide, y_offsets = call(
        widen_kernel, [((Z * PIECE, LANES), F32), ((Y, LANES), jnp.int32)], (offsets,), (lines,)
    )
    blocks = exchange(wide.reshape(Z, 1, PIECE * LANES), "pos_1").reshape(Z * PIECE, LANES)
    chosen, z_offsets = call(
        select_kernel,
        [((Y, CLASS_IN_PATCH, LANES), F32), ((Z, LANES), jnp.int32)],
        (y_offsets, me),
        (blocks,),
        ((PLANES, Y * Z, LANES),),
    )
    rows = exchange(chosen, "pos_0")
    packed = call(
        pack_kernel,
        (CHIPS, N, N),
        (offsets,),
        (rows, prop_phase.T, amplitude[0].T, probe_field),
        ((N, LANES),),
    )
    gathered = exchange(packed, "col_0")
    other = lax.ppermute(gathered, "col_1", [(0, 1), (1, 0)])
    grads = call(
        main_kernel,
        piece_shape,
        (offsets, counts, me),
        (gathered, other, jnp.asarray(dft_tables())),
        ((4, *halves), (2, *halves), (N, N), (2, N, N), (2, *halves), (2, *halves), (2, *halves), rows_shape),
        limit=24,
        extra=[pltpu.VMEM((6, N, N), BF16)],
    )
    returned = exchange(grads, "pos_1")
    summed = call(gather_kernel, fold_shape, (z_offsets, me), (returned,), (strip_shape,))
    tiles = exchange(summed, ("pos_0", "col_0", "col_1"))
    return call(
        merge_kernel, (2, 2, TILE, C * CLASS_IN_STRIP), (me,), (tiles,)
    )


COL = ("col_0", "col_1")


def solution(mesh):
    finer = Mesh(mesh.devices.reshape(Y, Z, CHIPS, CORES), POS + COL)
    return jax.shard_map(
        per_device,
        mesh=finer,
        in_specs=(
            P(None, None, POS, COL),
            P(None, COL, None),
            P(None, COL),
            P(POS, None, COL),
            P(POS, None),
            P(POS),
        ),
        out_specs=P(None, None, POS, COL),
        check_vma=False,
    )
```

```python
import math

import jax
import jax.numpy as jnp
import numpy as np
from jax import lax
from jax.experimental import pallas as pl
from jax.experimental.pallas import tpu as pltpu
from jax.sharding import Mesh
from jax.sharding import PartitionSpec as P

POS = ("pos_0", "pos_1")
MOD_FLOOR = 0.1

Y, Z, C = 8, 12, 8
CHIPS, CORES = 4, 2
N = 256
PLANES = 4
TILE = 8
CLASS_IN_STRIP = 12
STRIP = C * CLASS_IN_STRIP
PIECE = 26
CLASS_IN_PATCH = 32
TILES_PER_Z = 3
LANES = 128
CHUNK = 32
F32 = jnp.float32
SINE_SERIES = [(-1.0) ** k / math.factorial(2 * k + 1) for k in range(6)]
COSINE_SERIES = [(-1.0) ** k / math.factorial(2 * k) for k in range(7)]
BF16 = jnp.bfloat16


def exchange(x, axes):
    return lax.all_to_all(x, axes, 0, 0, tiled=True)


def class_order(shape, column_axis):
    column = lax.broadcasted_iota(jnp.int32, shape, column_axis)
    lane = lax.broadcasted_iota(jnp.int32, shape, 1 - column_axis)
    place = (column & (C - 1)) * 16 + lax.shift_right_logical(column, 3)
    return (place == lane).astype(F32)


def dft_tables():
    counter = np.arange(N)
    angle = (counter[:, None] * counter[None, :] % N) * (2.0 * np.pi / N)
    cosine, sine = np.cos(angle) / 16.0, np.sin(angle) / 16.0
    parts = []
    for table in (cosine, sine, -sine):
        table = table.astype(np.float32)
        high = table.astype(jnp.bfloat16)
        low = (table - high.astype(np.float32)).astype(jnp.bfloat16)
        parts += [high, low]
    return np.stack(parts)


def lanes():
    return lax.broadcasted_iota(jnp.int32, (TILE, LANES), 1)


def between(lane, low, width):
    return (lane >= low) & (lane < low + width)


def rolled(x, shift):
    if isinstance(shift, int):
        shift = shift % LANES
        return pltpu.roll(x, shift, 1) if shift else x
    return pltpu.roll(x, (shift + 2 * LANES) & (LANES - 1), 1)


def spread_masks(shift):
    lane = lanes()
    row = lax.broadcasted_iota(jnp.int32, (TILE, LANES), 0)
    base = lane - jnp.where(row < 4, 0, 16) - shift + 4 * LANES
    return [((base - 32 * p) & (LANES - 1)) < CLASS_IN_STRIP for p in range(PLANES)]


def upper_half():
    return lax.broadcasted_iota(jnp.int32, (TILE, LANES), 0) < 4


def folded(piece):
    return (piece + pltpu.roll(piece, 4, 0))[:4]


def unfolded(piece):
    return jnp.concatenate([piece, piece], axis=0)


def two_shifts(x, shift, low):
    return jnp.where(low, rolled(x, shift), rolled(x, shift + 16))


def split_kernel(me_ref, own_ref, x_ref, o_ref):
    shift = CLASS_IN_STRIP * me_ref[1]
    tile = x_ref[...].reshape(PLANES * TILE, C * CLASS_IN_STRIP)
    order = class_order((C * CLASS_IN_STRIP, LANES), 0)
    ordered = jnp.dot(
        tile, order, precision=lax.Precision.HIGHEST, preferred_element_type=F32
    )
    lane = lanes()
    base = lane - shift + 4 * LANES
    row, col = own_ref[0, 0].astype(F32), own_ref[0, 1].astype(F32)
    corner = jnp.where((base & (LANES - 1)) == CLASS_IN_STRIP, row, 0.0)
    corner = jnp.where((base & (LANES - 1)) == CLASS_IN_STRIP + 1, col, corner)
    for j in range(C):
        piece = corner
        for p in range(PLANES):
            moved = rolled(ordered[p * TILE : (p + 1) * TILE], shift + 32 * p - 16 * j)
            piece = jnp.where(((base - 32 * p) & (LANES - 1)) < CLASS_IN_STRIP, moved, piece)
        o_ref[j * TILE : (j + 1) * TILE] = piece


def widen_kernel(own_ref, x_ref, o_ref, off_ref):
    lane = lanes()
    planes = []
    for p in range(PLANES):
        line = x_ref[0:TILE]
        for j in range(1, C):
            inside = ((lane - CLASS_IN_STRIP * j - 32 * p + 2 * LANES) & (LANES - 1)) < CLASS_IN_STRIP
            line = jnp.where(inside, x_ref[j * TILE : (j + 1) * TILE], line)
        planes.append(rolled(line, -32 * p))
    packed = [
        jnp.where(lane < STRIP, planes[q], rolled(planes[3], STRIP - 32 * q)) for q in range(3)
    ]
    row, col = own_ref[0, 0].astype(F32), own_ref[0, 1].astype(F32)
    corner = jnp.where(lane[: PIECE - 3 * TILE] == 0, row, col)
    for z in range(Z):
        for q in range(3):
            o_ref[z * PIECE + q * TILE : z * PIECE + (q + 1) * TILE] = packed[q]
        o_ref[z * PIECE + 3 * TILE : (z + 1) * PIECE] = corner
    off_ref[...] = x_ref[0:TILE].astype(jnp.int32)


def window(off_ref, me_ref, z):
    row, col = off_ref[z, 0], off_ref[z, 1]
    z_me, c_me = me_ref[0], me_ref[1]
    first = lax.shift_right_logical(row, 3)
    ahead = lax.rem(z_me - first + 6 * Z, Z)
    y_first = lax.div(first + ahead - z_me, Z)
    u_first = lax.shift_right_logical(col - c_me + 7, 3)
    return y_first, u_first


def select_kernel(off_ref, me_ref, x_ref, o_ref, z_off_ref, strip_ref):
    lane = lanes()
    for z in range(Z):
        packed = [x_ref[z * PIECE + q * TILE : z * PIECE + (q + 1) * TILE] for q in range(3)]
        last = rolled(packed[2], 64 - STRIP)
        last = jnp.where(lane < 64, rolled(packed[1], 32 - STRIP), last)
        last = jnp.where(lane < 32, rolled(packed[0], -STRIP), last)
        for p, line in enumerate(packed + [last]):
            strip_ref[p, pl.ds(z, Y, stride=Z), :] = line
        z_off_ref[z : z + 1] = x_ref[z * PIECE + 3 * TILE : z * PIECE + 3 * TILE + 1].astype(jnp.int32)
    lane = lax.broadcasted_iota(jnp.int32, (CLASS_IN_PATCH, LANES), 1)
    for y in range(Y):
        row, col = off_ref[y, CLASS_IN_STRIP], off_ref[y, CLASS_IN_STRIP + 1]
        n_first = lax.shift_right_logical(row - me_ref[2] + 7, 3)
        u_first = lax.shift_right_logical(col - me_ref[1] + 7, 3)
        rows = pl.ds(n_first, CLASS_IN_PATCH)
        piece = rolled(strip_ref[0, rows, :], LANES - u_first)
        for p in range(1, PLANES):
            moved = rolled(strip_ref[p, rows, :], 32 * p - u_first)
            piece = jnp.where(lane >= 32 * p, moved, piece)
        o_ref[y] = piece


def pack_kernel(own_ref, x_ref, phase_ref, amp_ref, probe_ref, o_ref, rows_ref):
    row = own_ref[0, 0]
    for s in range(Y):
        rows_ref[pl.ds(s, CLASS_IN_PATCH, stride=Y), :] = x_ref[(row + s) & (Y - 1)]
    patch = rows_ref[...].T
    for copy in range(CHIPS):
        o_ref[copy, 0:128] = patch
        o_ref[copy, 128:160] = phase_ref[...]
        o_ref[copy, 160:192] = amp_ref[...]
        o_ref[copy, 192:224] = probe_ref[0]
        o_ref[copy, 224:256] = probe_ref[1]


def two_terms(x):
    high = x.astype(BF16)
    return high, (x - high.astype(F32)).astype(BF16)


def product(first, second):
    return jnp.dot(
        jnp.concatenate([first[0], first[0], first[1]], axis=1),
        jnp.concatenate([second[0], second[1], second[0]], axis=0),
        preferred_element_type=F32,
    )


def cosine_and_sine(angle):
    half = 0.5 * angle
    square = half * half
    sine = jnp.full_like(square, SINE_SERIES[-1])
    for coefficient in SINE_SERIES[-2::-1]:
        sine = sine * square + coefficient
    cosine = jnp.full_like(square, COSINE_SERIES[-1])
    for coefficient in COSINE_SERIES[-2::-1]:
        cosine = cosine * square + coefficient
    sine = sine * half
    twice = sine + sine
    return 1.0 - twice * sine, twice * cosine


def store(ref, at, value):
    ref[at, 0] = value[:, :LANES]
    ref[at, 1] = value[:, LANES:]


def load(ref, at, rows=slice(None)):
    return jnp.concatenate([ref[at, 0, rows, :], ref[at, 1, rows, :]], axis=1)


def main_kernel(
    own_ref, count_ref, me_ref, g_ref, other_ref, tab_ref, o_ref,
    patch_ref, h_ref, amp_ref, raw_ref, probe_ref, wave_ref, x_ref, rows_ref, op_ref,
):
    row, col = own_ref[0, 0], own_ref[0, 1]
    core = me_ref[1] & 1
    for source_ref, core_of in ((g_ref, core), (other_ref, 1 - core)):
        for chip in range(CHIPS):
            j = CORES * chip + core_of
            s = (j - col + 1024) & (C - 1)
            mine = pl.ds(pl.multiple_of(32 * j, 32), 32)
            amp_ref[mine, :] = source_ref[chip, 160:192, :]
            raw_ref[0, mine, :] = source_ref[chip, 192:224, :]
            raw_ref[1, mine, :] = source_ref[chip, 224:256, :]
            for half in range(2):
                part = slice(half * LANES, (half + 1) * LANES)
                for p in range(PLANES):
                    patch_ref[p, half, pl.ds(s, CLASS_IN_PATCH, stride=C), :] = source_ref[
                        chip, p * 32 : (p + 1) * 32, part
                    ]
    store(probe_ref, 0, raw_ref[0].T)
    store(probe_ref, 1, raw_ref[1].T)

    def table(k):
        return tab_ref[2 * k], tab_ref[2 * k + 1]

    def held(ref, at=0, rows=slice(None)):
        return load(ref, at, rows), load(ref, at + 1, rows)

    def keep(ref, pair):
        store(ref, 0, pair[0])
        store(ref, 1, pair[1])

    def keep_rows(ref, rows, pair):
        for at in range(2):
            ref[at, 0, rows] = pair[at][:, :LANES]
            ref[at, 1, rows] = pair[at][:, LANES:]

    def stage(inverse, left, rows=N):
        plus, minus = (2, 1) if inverse else (1, 2)

        def terms(at, k):
            data = (op_ref[at, :rows], op_ref[at + 1, :rows])
            return (table(k), data) if left else (data, table(k))

        def total(*pairs):
            return jnp.dot(
                jnp.concatenate([part for f, s in pairs for part in (f[0], f[0], f[1])], axis=1),
                jnp.concatenate([part for f, s in pairs for part in (s[0], s[1], s[0])], axis=0),
                preferred_element_type=F32,
            )

        if left:
            return total(terms(0, 0), terms(2, plus)), total(terms(2, 0), terms(0, minus))
        real = [op_ref[t, :rows] for t in (0, 1)]
        imag = [op_ref[2 + t, :rows] for t in (0, 1)]
        upper = [jnp.concatenate([table(0)[t], table(minus)[t]], axis=1) for t in (0, 1)]
        lower = [jnp.concatenate([table(plus)[t], table(0)[t]], axis=1) for t in (0, 1)]
        both = jnp.dot(
            jnp.concatenate([real[0], imag[0], real[0], imag[0], real[1], imag[1]], axis=1),
            jnp.concatenate([upper[0], lower[0], upper[1], lower[1], upper[0], lower[0]], axis=0),
            preferred_element_type=F32,
        )
        return both[:, :N], both[:, N:]

    def prepare(rows, pair):
        real, imag = pair
        for at, part in ((0, real), (2, imag)):
            op_ref[at, rows], op_ref[at + 1, rows] = two_terms(part)

    def chunks(step):
        for start in range(0, N, CHUNK):
            step(slice(start, start + CHUNK))

    def propagator():
        for source_ref, core_of in ((g_ref, core), (other_ref, 1 - core)):
            for chip in range(CHIPS):
                rows = pl.ds(pl.multiple_of(32 * (CORES * chip + core_of), 32), 32)
                keep_rows(h_ref, rows, cosine_and_sine(source_ref[chip, 128:160, :]))

    def transform(inverse, meanwhile=None):
        keep(x_ref, stage(inverse, True))
        if meanwhile:
            meanwhile()
        chunks(lambda rows: prepare(rows, held(x_ref, 0, rows)))
        keep(x_ref, stage(inverse, False))

    def times(a, b):
        return a[0] * b[0] - a[1] * b[1], a[0] * b[1] + a[1] * b[0]

    def conj_times(a, b):
        return a[0] * b[0] + a[1] * b[1], a[0] * b[1] - a[1] * b[0]

    def enter(rows):
        prepare(rows, times(held(probe_ref, 0, rows), held(patch_ref, 0, rows)))

    def propagate(rows):
        prepare(rows, times(held(h_ref, 0, rows), held(x_ref, 0, rows)))

    def modulate(rows):
        wave = held(x_ref, 0, rows)
        keep_rows(wave_ref, rows, wave)
        prepare(rows, times(wave, held(patch_ref, 2, rows)))

    def correct(rows):
        real, imag = held(x_ref, 0, rows)
        modulus = jnp.maximum(jnp.sqrt(real * real + imag * imag), MOD_FLOOR)
        ratio = amp_ref[rows] / modulus
        prepare(rows, (real - ratio * real, imag - ratio * imag))

    def turn_back(rows):
        back = held(x_ref, 0, rows)
        keep_rows(wave_ref, rows, conj_times(held(wave_ref, 0, rows), back))
        prepare(rows, conj_times(held(patch_ref, 2, rows), back))

    def propagate_back(rows):
        prepare(rows, conj_times(held(h_ref, 0, rows), held(x_ref, 0, rows)))

    chunks(enter)
    transform(False, propagator)
    chunks(propagate)
    transform(True)
    chunks(modulate)
    transform(False)
    chunks(correct)
    transform(True)
    chunks(turn_back)
    transform(False)
    chunks(propagate_back)
    keep(x_ref, stage(True, True))
    mine = pl.ds((me_ref[1] - col + 1024) & (C - 1), CLASS_IN_PATCH, stride=C)
    prepare(slice(0, CLASS_IN_PATCH), held(x_ref, 0, mine))
    back = stage(True, False, CLASS_IN_PATCH)
    first_grad = conj_times(held(probe_ref, 0, mine), back)
    second_grad = held(wave_ref, 0, mine)
    alive = (count_ref[0] > 0).astype(F32)
    grads = jnp.concatenate([*first_grad, *second_grad], axis=0) * alive
    rows_ref[...] = jnp.zeros_like(rows_ref)
    rows_ref[pl.ds(row & 7, N), :] = grads.T
    first = lax.shift_right_logical(row, 3)
    for m in range(Z * TILES_PER_Z):
        k = m // Z
        o_ref[lax.rem(first + m, Z), k * TILE : (k + 1) * TILE] = rows_ref[
            m * TILE : (m + 1) * TILE
        ]


def gather_kernel(off_ref, me_ref, x_ref, o_ref, sum_ref):
    lane = lanes()
    sum_ref[...] = jnp.zeros_like(sum_ref)
    for z in range(Z):
        y_first, u_first = window(off_ref, me_ref, z)
        inside = between(lane, u_first, CLASS_IN_PATCH)
        for k in range(TILES_PER_Z):
            piece = x_ref[z, k * TILE : (k + 1) * TILE]
            for p in range(PLANES):
                moved = jnp.where(inside, rolled(piece, u_first - 32 * p), 0.0)
                sum_ref[p, y_first + k] += moved
    masks, low = [spread_masks(CLASS_IN_STRIP * j) for j in range(C)], upper_half()
    for y in range(Y):
        lines = [two_shifts(sum_ref[p, y], 32 * p, low) for p in range(PLANES)]
        for j in range(C):
            piece = jnp.zeros((TILE, LANES), F32)
            for p in range(PLANES):
                piece = jnp.where(masks[j][p], lines[p], piece)
            o_ref[y * C + j] = folded(piece)


def merge_kernel(me_ref, x_ref, o_ref):
    lane, low = lanes(), upper_half()
    shift = CLASS_IN_STRIP * me_ref[1]
    sums = []
    for j in range(C):
        total = x_ref[j]
        for y in range(1, Y):
            total = total + x_ref[y * C + j]
        sums.append(unfolded(total))
    planes = []
    for p in range(PLANES):
        line = jnp.zeros((TILE, LANES), F32)
        for j in range(C):
            start = 16 * j - shift - 32 * p
            moved = jnp.where(low, rolled(sums[j], start), rolled(sums[j], start - 16))
            line = jnp.where(between(lane, 16 * j, CLASS_IN_STRIP), moved, line)
        planes.append(line)
    ordered = jnp.concatenate(planes, axis=0)
    order = class_order((LANES, C * CLASS_IN_STRIP), 1)
    tile = jnp.dot(
        ordered, order, precision=lax.Precision.HIGHEST, preferred_element_type=F32
    )
    o_ref[...] = tile.reshape(2, 2, TILE, C * CLASS_IN_STRIP)


IN_VMEM = pl.BlockSpec(memory_space=pltpu.VMEM)
IN_SMEM = pl.BlockSpec(memory_space=pltpu.SMEM)


def call(kernel, out_shape, scalars, arrays, scratch=(), limit=8, extra=()):
    single = isinstance(out_shape, tuple)
    outs = [jax.ShapeDtypeStruct(*out) for out in ([(out_shape, F32)] if single else out_shape)]
    return pl.pallas_call(
        kernel,
        out_shape=outs[0] if single else outs,
        in_specs=[IN_SMEM] * len(scalars) + [IN_VMEM] * len(arrays),
        out_specs=IN_VMEM if single else [IN_VMEM] * len(outs),
        scratch_shapes=[pltpu.VMEM(shape, F32) for shape in scratch] + list(extra),
        compiler_params=pltpu.CompilerParams(vmem_limit_bytes=limit * 1024 * 1024),
    )(*scalars, *arrays)


def per_device(object_layers, probe_field, prop_phase, amplitude, offsets, counts):
    strip_shape = (PLANES, Y + 1, TILE, LANES)
    fold_shape = (Y * C, TILE // 2, LANES)
    piece_shape = (Z, TILES_PER_Z * TILE, LANES)
    rows_shape = (Z * TILES_PER_Z * TILE + TILE, LANES)
    halves = (2, N, LANES)
    col_at = lax.axis_index("col_0") * CORES + lax.axis_index("col_1")
    me = jnp.stack([lax.axis_index("pos_1"), col_at, lax.axis_index("pos_0")]).astype(jnp.int32)
    split = call(split_kernel, (C * TILE, LANES), (me, offsets), (object_layers,))
    lines = exchange(split.reshape(C * Y, 1, LANES), COL + ("pos_0",)).reshape(C * Y, LANES)
    wide, y_offsets = call(
        widen_kernel, [((Z * PIECE, LANES), F32), ((Y, LANES), jnp.int32)], (offsets,), (lines,)
    )
    blocks = exchange(wide.reshape(Z, 1, PIECE * LANES), "pos_1").reshape(Z * PIECE, LANES)
    chosen, z_offsets = call(
        select_kernel,
        [((Y, CLASS_IN_PATCH, LANES), F32), ((Z, LANES), jnp.int32)],
        (y_offsets, me),
        (blocks,),
        ((PLANES, Y * Z, LANES),),
    )
    rows = exchange(chosen, "pos_0")
    packed = call(
        pack_kernel,
        (CHIPS, N, N),
        (offsets,),
        (rows, prop_phase.T, amplitude[0].T, probe_field),
        ((N, LANES),),
    )
    gathered = exchange(packed, "col_0")
    other = lax.ppermute(gathered, "col_1", [(0, 1), (1, 0)])
    grads = call(
        main_kernel,
        piece_shape,
        (offsets, counts, me),
        (gathered, other, jnp.asarray(dft_tables())),
        ((4, *halves), (2, *halves), (N, N), (2, N, N), (2, *halves), (2, *halves), (2, *halves), rows_shape),
        limit=24,
        extra=[pltpu.VMEM((4, N, N), BF16)],
    )
    returned = exchange(grads, "pos_1")
    summed = call(gather_kernel, fold_shape, (z_offsets, me), (returned,), (strip_shape,))
    tiles = exchange(summed, ("pos_0", "col_0", "col_1"))
    return call(
        merge_kernel, (2, 2, TILE, C * CLASS_IN_STRIP), (me,), (tiles,)
    )


COL = ("col_0", "col_1")


def solution(mesh):
    finer = Mesh(mesh.devices.reshape(Y, Z, CHIPS, CORES), POS + COL)
    return jax.shard_map(
        per_device,
        mesh=finer,
        in_specs=(
            P(None, None, POS, COL),
            P(None, COL, None),
            P(None, COL),
            P(POS, None, COL),
            P(POS, None),
            P(POS),
        ),
        out_specs=P(None, None, POS, COL),
        check_vma=False,
    )
```
